32 devices in a mesh: dp: 8 (over z, x), neg: 4 (over y, core).
Axes of the slice: x: 2, y: 2, z: 4, core: 2. Of those that a mesh axis runs over, the one named last changes fastest.
Arguments:
- history: bfloat16 [6144, 512], P('dp'), may hold values from -6 to 6
- lengths: int32 [16], P('dp'), may hold values from 1 to 384
- w_in: bfloat16 [512, 2048], P(None, 'neg'), may hold values from -0.25 to 0.25
- w_out: bfloat16 [512, 512], P('neg'), may hold values from -0.25 to 0.25
- target_ids: int32 [6144], P('dp'), may hold values from 0 to 8191
- negative_ids: int32 [16384], P('neg'), may hold values from 0 to 8191, as said below
- item_table: bfloat16 [8192, 512], P('neg'), may hold values from -6 to 6
Outputs:
- token_loss: float32 [6144], P('dp')
- grad_w_in: float32 [512, 2048], P('dp', 'neg')
- grad_w_out: float32 [512, 512], P('neg', 'dp')
- grad_table: float32 [8192, 512], P(('neg', 'dp'))
The draws below stay inside these ranges and needn't reach their ends.
Inputs may be any that keep to these rules, and one draw needn't show every extreme that they name: `negative_ids`: negative n names one of the rows (n // 4096) * 2048 to (n // 4096 + 1) * 2048 - 1.
All inputs are finite; a program needn't handle non-finite values.
Results may differ from the reference program's by a relative error of at most 0.0098.
Values may be sent and summed in bfloat16 or wider, within the bound.
A program may use at most 128 MiB of HBM per device.

```python
import jax
import jax.numpy as jnp
from jax import lax

D = 512
HEADS = 8
HEAD = 64
NEG = 16384
ITEM_DEV = 2048
HIST = 384
USERS = 16
TOKENS = 6144
NEG_DEV = 4096
ITEMS = 8192


def draw_negative_ids(key, part):
    offsets = jax.random.randint(key, (NEG,), 0, ITEM_DEV, dtype=jnp.int32)
    owner = jnp.arange(NEG, dtype=jnp.int32) // NEG_DEV
    return (owner * ITEM_DEV + offsets).astype(jnp.int32)


def plant(result, own_key, low, high):
    shape = result.shape
    spot = [jax.random.randint(jax.random.fold_in(own_key, axis), (), 0, shape[axis]) for axis in range(len(shape))]
    result = result.at[tuple(spot)].set(low)
    longest = shape.index(max(shape))
    spot[longest] = (spot[longest] + 1) % shape[longest]
    return result.at[tuple(spot)].set(high)


def steps_of(stream_key, shape, shards, least, top_value):
    def one(dim, shards_of):
        steps = jax.random.uniform(jax.random.fold_in(jax.random.fold_in(stream_key, 6), dim), (shards_of,), jnp.float32, least / len(shards), top_value / len(shards))
        return jnp.repeat(jnp.exp(steps), shape[dim] // shards_of).reshape((-1,) + (1,) * (len(shape) - dim - 1))

    level = one(*shards[0])
    for cut in shards[1:]:
        level = level * one(*cut)
    return level


def gaussian(rng, shape, width, limit, pieces=(), kind=jnp.bfloat16):
    entries = jax.random.normal(rng, shape, jnp.float32) * width
    if len(pieces) > 0:
        entries = steps_of(rng, shape, pieces, -0.22, 0.18) * entries
    return jnp.clip(entries, min=-limit, max=limit).astype(kind)


def setup_inputs(seed: int = 0) -> dict:
    keys = jax.random.split(jax.random.key(seed), 8)
    history = gaussian(keys[0], (TOKENS, D), 1.0, 6.0, ((0, 8),))
    lengths = plant(jax.random.randint(keys[1], (USERS,), 1, HIST + 1), jax.random.fold_in(keys[1], 1), 1, HIST).astype(jnp.int32)
    w_in = gaussian(keys[2], (D, 4 * D), D ** -0.5, 0.25, ((1, 4),))
    w_out = gaussian(keys[3], (D, D), D ** -0.5, 0.25, ((0, 4),))
    target_ids = plant(jax.random.randint(keys[4], (TOKENS,), 0, ITEMS), jax.random.fold_in(keys[4], 1), 0, ITEMS - 1).astype(jnp.int32)
    negative_ids = draw_negative_ids(jax.random.fold_in(keys[7], 71), 0)
    item_table = gaussian(keys[6], (ITEMS, D), 1.0, 6.0, ((0, 4),))
    return {"history": history, "lengths": lengths, "w_in": w_in, "w_out": w_out, "target_ids": target_ids, "negative_ids": negative_ids, "item_table": item_table}


logit_scale = 64.0
epsilon = 1e-06

def product(left, right):
    return jnp.dot(left.astype(jnp.float32), right.astype(jnp.float32), precision=lax.Precision.HIGHEST)

def to_half(values):
    return lax.optimization_barrier(values.astype(jnp.bfloat16))

def silu_grad(values):
    logistic = jax.nn.sigmoid(values)
    return logistic * (1.0 + values * (1.0 - logistic))

def moment_norm(values):
    row_mean = lax.optimization_barrier(jnp.mean(values, -1, keepdims=True))
    row_square = lax.optimization_barrier(jnp.mean(values * values, -1, keepdims=True))
    norm_scale = lax.rsqrt(row_square - row_mean * row_mean + epsilon)
    return ((values - row_mean) * norm_scale, norm_scale)

def normalize_rows(values):
    inverse = lax.rsqrt(lax.optimization_barrier(jnp.sum(values * values, -1, keepdims=True)) + epsilon)
    return (values * inverse, inverse)

def reference(history, lengths, w_in, w_out, target_ids, negative_ids, item_table):
    item_unit, item_inverse = normalize_rows(item_table.astype(jnp.float32))
    item_rounded = to_half(item_unit)
    neg_rounded = item_rounded[negative_ids]
    position = jnp.arange(HIST, dtype=jnp.int32)
    causal = position[None, :] <= position[:, None]
    highest = lax.Precision.HIGHEST

    def one_user(scan_carry, user_data):
        grad_in_sum, grad_out_sum, neg_raw_sum = scan_carry
        user_rows, user_length, user_ids = user_data
        inputs_float = user_rows.astype(jnp.float32)
        normed = to_half(moment_norm(inputs_float)[0])
        pre_act = product(normed, w_in)
        projected = to_half(jax.nn.silu(pre_act)).astype(jnp.float32).reshape(HIST, HEADS, 4, HEAD)
        gate_rows = projected[:, :, 0]
        value_rows = projected[:, :, 1]
        query_rows = projected[:, :, 2]
        key_rows = projected[:, :, 3]
        scores = jnp.einsum('ihd,jhd->hij', query_rows, key_rows, precision=highest)
        live_rows = (position < user_length).astype(jnp.float32)
        attn_mask = (causal & (position < user_length)[:, None]).astype(jnp.float32)
        attn_weights = to_half(jax.nn.silu(scores) * attn_mask / HIST).astype(jnp.float32)
        attended = jnp.einsum('hij,jhd->ihd', attn_weights, value_rows, precision=highest).reshape(HIST, D)
        centred, norm_scale = moment_norm(attended)
        gate_flat = gate_rows.reshape(HIST, D)
        mixed_rows = to_half(centred * gate_flat)
        output = inputs_float + product(mixed_rows, w_out)
        user_unit, user_inverse = normalize_rows(output)
        user_rounded = to_half(user_unit)
        user_float = user_rounded.astype(jnp.float32)
        target_unit = item_unit[user_ids]
        positive = logit_scale * lax.optimization_barrier(jnp.sum(user_float * target_unit, -1))
        logits = logit_scale * product(user_rounded, neg_rounded.T)
        exp_terms = jnp.where(user_ids[:, None] != negative_ids[None, :], jnp.exp(logits), 0.0)
        partition_sum = jnp.exp(positive) + lax.optimization_barrier(jnp.sum(exp_terms, -1))
        token_loss = live_rows * (jnp.log(partition_sum) - positive)
        logit_grads = to_half(live_rows[:, None] * exp_terms / partition_sum[:, None])
        positive_grad = live_rows * (jnp.exp(positive) / partition_sum - 1.0)
        neg_raw = logit_scale * product(logit_grads.T, user_rounded)
        target_raw = logit_scale * positive_grad[:, None] * user_float
        unit_grad = logit_scale * product(logit_grads, neg_rounded) + logit_scale * positive_grad[:, None] * target_unit
        output_grad = to_half((unit_grad - user_unit * lax.optimization_barrier(jnp.sum(unit_grad * user_unit, -1, keepdims=True))) * user_inverse)
        grad_out = product(mixed_rows.T, output_grad)
        mixed_grad = product(output_grad, w_out.T)
        centred_grad = mixed_grad * gate_flat
        gate_grad = mixed_grad * centred
        attended_grad = norm_scale * (centred_grad - lax.optimization_barrier(jnp.mean(centred_grad, -1, keepdims=True)) - centred * lax.optimization_barrier(jnp.mean(centred_grad * centred, -1, keepdims=True)))
        attended_grad = to_half(attended_grad).astype(jnp.float32).reshape(HIST, HEADS, HEAD)
        weight_grad = jnp.einsum('ihd,jhd->hij', attended_grad, value_rows, precision=highest)
        value_grad = jnp.einsum('hij,ihd->jhd', attn_weights, attended_grad, precision=highest)
        score_grad = to_half(weight_grad * attn_mask / HIST * silu_grad(scores)).astype(jnp.float32)
        query_grad = jnp.einsum('hij,jhd->ihd', score_grad, key_rows, precision=highest)
        key_grad = jnp.einsum('hij,ihd->jhd', score_grad, query_rows, precision=highest)
        project_grad = jnp.stack([gate_grad.reshape(HIST, HEADS, HEAD), value_grad, query_grad, key_grad], 2).reshape(HIST, 4 * D)
        pre_grad = to_half(project_grad * silu_grad(pre_act))
        grad_in = product(normed.T, pre_grad)
        return ((grad_in_sum + grad_in, grad_out_sum + grad_out, neg_raw_sum + neg_raw), (token_loss, target_raw))
    start_carry = (jnp.zeros((D, 4 * D), jnp.float32), jnp.zeros((D, D), jnp.float32), jnp.zeros((NEG, D), jnp.float32))
    user_inputs = (history.reshape(USERS, HIST, D), lengths, target_ids.reshape(USERS, HIST))
    final_carry, stacked = lax.scan(one_user, start_carry, user_inputs)
    grad_w_in, grad_w_out, neg_raw_sum = final_carry
    token_loss = stacked[0].reshape(TOKENS)
    target_raws = stacked[1].reshape(TOKENS, D)
    row_grad = jax.ops.segment_sum(neg_raw_sum, negative_ids, ITEMS) + jax.ops.segment_sum(target_raws, target_ids, ITEMS)
    grad_table = (row_grad - item_unit * lax.optimization_barrier(jnp.sum(row_grad * item_unit, -1, keepdims=True))) * item_inverse
    return (token_loss, grad_w_in, grad_w_out, grad_table)
```

```python
import jax
import jax.numpy as jnp
from jax import lax
from jax.sharding import PartitionSpec as P

HEAD = 64


logit_scale = 64.0
epsilon = 1e-06


def silu_grad(values):
    logistic = jax.nn.sigmoid(values)
    return logistic * (1.0 + values * (1.0 - logistic))


def moment_norm(values):
    row_mean = jnp.mean(values, -1, keepdims=True)
    row_square = jnp.mean(values * values, -1, keepdims=True)
    norm_scale = lax.rsqrt(row_square - row_mean * row_mean + epsilon)
    return ((values - row_mean) * norm_scale, norm_scale)


def normalize_rows(values):
    inverse = lax.rsqrt(jnp.sum(values * values, -1, keepdims=True) + epsilon)
    return (values * inverse, inverse)


def project_rows(raw_rows, unit_part, inverse):
    return (raw_rows - unit_part * jnp.sum(raw_rows * unit_part, -1, keepdims=True)) * inverse


def count_rows(slots, row_count):
    lanes = 128
    coarse = (slots // lanes)[None, :] == jnp.arange(row_count // lanes, dtype=jnp.int32)[:, None]
    fine = (slots % lanes)[:, None] == jnp.arange(lanes, dtype=jnp.int32)[None, :]
    table = jnp.dot(
        coarse.astype(jnp.bfloat16), fine.astype(jnp.bfloat16), preferred_element_type=jnp.float32
    )
    return table.reshape(1, row_count)


def on_device(history, lengths, w_in, w_out, target_ids, negative_ids, item_table):
    tok_rows, model_width = history.shape
    user_count = lengths.shape[0]
    hist_len = tok_rows // user_count
    local_heads = w_in.shape[1] // (4 * HEAD)
    local_width = local_heads * HEAD
    item_rows = item_table.shape[0]
    groups = lax.axis_size("neg")
    share_rows = tok_rows // groups
    share_start = lax.axis_index("neg") * share_rows
    item_base = lax.axis_index("neg") * item_rows
    inputs_float = history.astype(jnp.float32)
    normed = moment_norm(inputs_float)[0].astype(jnp.bfloat16)
    pre_act = jnp.dot(normed, w_in, preferred_element_type=jnp.float32)
    projected = (
        jax.nn.silu(pre_act)
        .astype(jnp.bfloat16)
        .reshape(user_count, hist_len, local_heads, 4, HEAD)
    )
    gate_rows = projected[:, :, :, 0]
    value_rows = projected[:, :, :, 1]
    query_rows = projected[:, :, :, 2]
    key_rows = projected[:, :, :, 3]
    scores = jnp.einsum("bihd,bjhd->bhij", query_rows, key_rows, preferred_element_type=jnp.float32)
    position = jnp.arange(hist_len, dtype=jnp.int32)
    live_slots = position[None, :] < lengths[:, None]
    causal = position[None, :] <= position[:, None]
    attn_mask = (causal[None] & live_slots[:, :, None]).astype(jnp.float32)[:, None]
    attn_weights = (jax.nn.silu(scores) * attn_mask / hist_len).astype(jnp.bfloat16)
    attended = jnp.einsum(
        "bhij,bjhd->bihd", attn_weights, value_rows, preferred_element_type=jnp.float32
    ).reshape(tok_rows, local_width)
    head_sums = lax.psum((jnp.sum(attended, -1), jnp.sum(attended * attended, -1)), "neg")
    row_mean = head_sums[0][:, None] / model_width
    norm_scale = lax.rsqrt(head_sums[1][:, None] / model_width - row_mean * row_mean + epsilon)
    centred = (attended - row_mean) * norm_scale
    gate_flat = gate_rows.reshape(tok_rows, local_width).astype(jnp.float32)
    mixed_rows = (centred * gate_flat).astype(jnp.bfloat16)
    branch = jnp.dot(mixed_rows, w_out, preferred_element_type=jnp.float32)
    branch_part = lax.psum_scatter(
        branch.astype(jnp.bfloat16), "neg", scatter_dimension=0, tiled=True
    ).astype(jnp.float32)
    inputs_part = lax.dynamic_slice_in_dim(inputs_float, share_start, share_rows, 0)
    user_unit, user_inverse = normalize_rows(inputs_part + branch_part)
    user_rounded = lax.all_gather(user_unit.astype(jnp.bfloat16), "neg", axis=0, tiled=True)
    item_unit, item_inverse = normalize_rows(item_table.astype(jnp.float32))
    item_rounded = item_unit.astype(jnp.bfloat16)
    row_counts = count_rows(negative_ids - item_base, item_rows)
    is_target = (target_ids - item_base)[:, None] == jnp.arange(item_rows, dtype=jnp.int32)[None, :]
    logits = logit_scale * lax.dot_general(
        user_rounded, item_rounded, (((1,), (1,)), ((), ())), preferred_element_type=jnp.float32
    )
    exp_terms = jnp.where(is_target, 0.0, row_counts * jnp.exp(logits))
    positive, negative_sum = lax.psum(
        (jnp.sum(jnp.where(is_target, logits, 0.0), -1), jnp.sum(exp_terms, -1)), "neg"
    )
    partition_sum = jnp.exp(positive) + negative_sum
    live_rows = live_slots.reshape(tok_rows).astype(jnp.float32)
    token_loss = live_rows * (jnp.log(partition_sum) - positive)
    positive_grad = live_rows * (jnp.exp(positive) / partition_sum - 1.0)
    row_factor = live_rows / partition_sum
    coefficients = jnp.where(
        is_target, positive_grad[:, None], row_factor[:, None] * exp_terms
    ).astype(jnp.bfloat16)
    unit_part = logit_scale * jnp.dot(
        coefficients, item_rounded, preferred_element_type=jnp.float32
    )
    row_raw = logit_scale * lax.dot_general(
        coefficients, user_rounded, (((0,), (0,)), ((), ())), preferred_element_type=jnp.float32
    )
    row_total = lax.psum_scatter(
        row_raw.astype(jnp.bfloat16), "dp", scatter_dimension=0, tiled=True
    ).astype(jnp.float32)
    unit_grad = lax.psum_scatter(
        unit_part.astype(jnp.bfloat16), "neg", scatter_dimension=0, tiled=True
    ).astype(jnp.float32)
    output_part = project_rows(unit_grad, user_unit, user_inverse).astype(jnp.bfloat16)
    output_rounded = lax.all_gather(output_part, "neg", axis=0, tiled=True)
    grad_out_local = lax.dot_general(
        output_rounded, mixed_rows, (((0,), (0,)), ((), ())), preferred_element_type=jnp.float32
    )
    mixed_grad = lax.dot_general(
        output_rounded, w_out, (((1,), (1,)), ((), ())), preferred_element_type=jnp.float32
    )
    centred_grad = mixed_grad * gate_flat
    gate_grad = mixed_grad * centred
    back_sums = lax.psum((jnp.sum(centred_grad, -1), jnp.sum(centred_grad * centred, -1)), "neg")
    attended_grad = norm_scale * (
        centred_grad
        - back_sums[0][:, None] / model_width
        - centred * back_sums[1][:, None] / model_width
    )
    attended_grad = attended_grad.astype(jnp.bfloat16).reshape(
        user_count, hist_len, local_heads, HEAD
    )
    weight_grad = jnp.einsum(
        "bihd,bjhd->bhij", attended_grad, value_rows, preferred_element_type=jnp.float32
    )
    value_grad = jnp.einsum(
        "bhij,bihd->bjhd", attn_weights, attended_grad, preferred_element_type=jnp.float32
    )
    score_grad = (weight_grad * attn_mask / hist_len * silu_grad(scores)).astype(jnp.bfloat16)
    query_grad = jnp.einsum(
        "bhij,bjhd->bihd", score_grad, key_rows, preferred_element_type=jnp.float32
    )
    key_grad = jnp.einsum(
        "bhij,bihd->bjhd", score_grad, query_rows, preferred_element_type=jnp.float32
    )
    project_grad = jnp.stack(
        [
            gate_grad.reshape(user_count, hist_len, local_heads, HEAD),
            value_grad,
            query_grad,
            key_grad,
        ],
        3,
    ).reshape(tok_rows, 4 * local_width)
    pre_grad = (project_grad * silu_grad(pre_act)).astype(jnp.bfloat16)
    grad_in_local = lax.dot_general(
        normed, pre_grad, (((0,), (0,)), ((), ())), preferred_element_type=jnp.float32
    )
    grad_w_in = lax.psum_scatter(
        grad_in_local.astype(jnp.bfloat16), "dp", scatter_dimension=0, tiled=True
    ).astype(jnp.float32)
    grad_w_out = (
        lax.psum_scatter(
            grad_out_local.astype(jnp.bfloat16), "dp", scatter_dimension=0, tiled=True
        )
        .astype(jnp.float32)
        .T
    )
    table_share = item_rows // lax.axis_size("dp")
    own_first = lax.axis_index("dp") * table_share
    grad_table = project_rows(
        row_total,
        lax.dynamic_slice_in_dim(item_unit, own_first, table_share, 0),
        lax.dynamic_slice_in_dim(item_inverse, own_first, table_share, 0),
    )
    return (token_loss, grad_w_in, grad_w_out, grad_table)


def solution(mesh):
    placed = (
        P("dp", None),
        P("dp"),
        P(None, "neg"),
        P("neg", None),
        P("dp"),
        P("neg"),
        P("neg", None),
    )
    return jax.shard_map(
        on_device,
        mesh=mesh,
        in_specs=placed,
        out_specs=(P("dp"), P("dp", "neg"), P("neg", "dp"), P(("neg", "dp"), None)),
        check_vma=False,
    )
```
